32 devices in a mesh: expert: 16 (over z, y, x), replica: 2 (over core).
Axes of the slice: x: 2, y: 2, z: 4, core: 2. Of those that a mesh axis runs over, the one named last changes fastest.
Arguments:
- tokens: bfloat16 [2048, 7168], P('expert', 'replica'), may hold values from -6 to 6
- gate_weight: bfloat16 [16, 7168, 1024], P('expert', 'replica'), may hold values from -0.0625 to 0.0625
- routes: int32 [2048, 8], P('expert'), may hold values from 0 to 15, all different within a row; in each aligned block of 128 rows (0 to 127, 128 to 255, ...) at most 80 rows name the same one
- combine: bfloat16 [2048, 8], P('expert'), may hold values from 0.099609375 to 1
- cotangent: bfloat16 [2048, 8, 1024], P('expert', None, 'replica'), may hold values from -1.5 to 1.5
Outputs:
- token_grad: bfloat16 [2048, 7168], P('expert', 'replica')
- weight_grad: bfloat16 [16, 7168, 1024], P('expert', 'replica')
The draws below stay inside these ranges and needn't reach their ends.
Inputs may be any that keep to these rules, and one draw needn't show every extreme that they name: `routes`: each row names 8 different experts. Among the 128 rows of one index of expert (aligned blocks), no expert is named more than 80 times, and in every draw some expert is named exactly 80 times in some block.
All inputs are finite; a program needn't handle non-finite values.
Results may differ from the reference program's by a relative error of at most 0.013.
Values may be sent and summed in bfloat16 or wider, within the bound.
A program may use at most 128 MiB of HBM per device.

```python
import math
import jax
import jax.numpy as jnp
import numpy as np
from jax import lax

D = 7168
TOPK = 8
HW = 1024
TOK_DEV = 128
EXPERTS = 16
CAP = 80
TOKENS = 2048
N_EXPERT = 16
N_REPLICA = 2


def steps_of(key, shape, pieces, smallest, top_value):
    loudness = 1.0
    for dim, shards_of in pieces:
        steps = jax.random.uniform(jax.random.fold_in(jax.random.fold_in(key, 6), dim), (shards_of,), jnp.float32, smallest / len(pieces), top_value / len(pieces))
        loudness = loudness * jnp.repeat(jnp.exp(steps), shape[dim] // shards_of).reshape((-1,) + (1,) * (len(shape) - 1 - dim))
    return loudness


def shared_out(key, own, number, rows, number_of, top, bound, skew):
    ranking = jax.random.permutation(key, number_of)
    crowded, ordinary = load_shares(number_of, rows * top, bound, skew, True), load_shares(number_of, rows * top, bound, skew, False)
    places = jnp.arange(number_of)

    def named(lengths, offset_by):
        used = int((lengths > 0).sum())
        fixed = max(1, used // 4)
        shifted = fixed + (places - fixed + offset_by * (used - fixed)) % max(1, number_of - fixed)
        return jnp.zeros((number_of,), jnp.int32).at[ranking[jnp.where(places < fixed, places, shifted)]].set(jnp.asarray(lengths, jnp.int32))

    lengths = jnp.where(number % 4 == 0, named(crowded, number // 4), named(ordinary, number - number // 4 - 1))
    mixed = jax.random.permutation(jax.random.fold_in(own, 3), number_of)
    giver, taker = mixed[0:number_of // 2 * 2:2], mixed[1:number_of // 2 * 2:2]
    slack = jnp.minimum(lengths[giver] - 1, bound - lengths[taker]) // 2
    slack = jnp.where((giver == ranking[0]) | (taker == ranking[0]) | (lengths[taker] == 0), 0, jnp.maximum(slack, 0))
    shifted = jax.random.randint(jax.random.fold_in(own, 4), (number_of // 2,), 0, 1 << 20) % (slack + 1)
    lengths = lengths.at[giver].add(-shifted).at[taker].add(shifted)
    members = jnp.searchsorted(jnp.cumsum(lengths), jnp.arange(rows * top), side="right").astype(jnp.int32)
    table = members.reshape(top, rows).T
    table = table[jax.random.permutation(jax.random.fold_in(own, 1), rows)]
    offset_by = jax.random.randint(jax.random.fold_in(own, 2), (rows, 1), 0, top)
    return jnp.take_along_axis(table, (jnp.arange(top)[None, :] + offset_by) % top, axis=1)


def load_shares(number_of, total, reach, slope, full):
    portions = [(1 << 20) // math.isqrt(standing ** slope) + 1 for standing in range(1, number_of + 1)]
    largest = reach if full else min(reach, max(-(-total // number_of), total * portions[0] // sum(portions)))
    least = 1 if total - largest >= number_of - 1 else 0
    holding, spare = [largest] + [least] * (number_of - 1), total - largest - least * (number_of - 1)
    while spare > 0:
        movable = [i for i in range(1, number_of) if holding[i] < largest] or [i for i in range(1, number_of) if holding[i] < reach]
        whole, remaining = sum([portions[i] for i in movable]), spare
        for i in movable:
            addition = min(reach - holding[i], max(1, remaining * portions[i] // whole), spare)
            holding[i] = holding[i] + addition
            spare = spare - addition
    return np.array(holding)


def gaussian(own_key, shape, scale, most, split=(), kind=jnp.bfloat16):
    level = steps_of(own_key, shape, split, -0.22, 0.18) if split else 1.0
    array = jax.random.normal(own_key, shape, jnp.float32) * scale * level
    return jnp.minimum(jnp.maximum(array, -most), most).astype(kind)


def setup_inputs(seed: int = 0) -> dict:
    key_list = jax.random.split(jax.random.key(seed), 6)
    tokens = gaussian(key_list[0], (TOKENS, D), 1.0, 6.0, ((0, 16), (1, 2)))
    gate_weight = gaussian(key_list[1], (EXPERTS, D, HW), D ** -0.5, 0.0625, ((0, 16), (1, 2)))
    routes_keys = jax.random.split(jax.random.fold_in(key_list[2], 1), TOKENS // TOK_DEV)
    routes_turns = jax.random.permutation(jax.random.fold_in(key_list[2], 3), TOKENS // TOK_DEV)
    routes = jax.vmap(lambda own, number: shared_out(jax.random.fold_in(key_list[2], 2), own, number, TOK_DEV, EXPERTS, TOPK, CAP, 2))(routes_keys, routes_turns).reshape((TOKENS, TOPK))
    combine = jnp.clip(0.099609375 + 0.9003906 * jax.random.uniform(key_list[3], (TOKENS, TOPK), jnp.float32) ** steps_of(key_list[3], (TOKENS, TOPK), ((0, 16),), -0.2, 0.2), 0.099609375, 1.0).astype(jnp.bfloat16)
    cotangent = gaussian(key_list[4], (TOKENS, TOPK, HW), 0.25, 1.5, ((0, 16), (2, 2)))
    return dict(tokens=tokens, gate_weight=gate_weight, routes=routes, combine=combine, cotangent=cotangent)


def silu_slope(gate):
    sig = jax.nn.sigmoid(gate)
    return sig * (1.0 + gate * (1.0 - sig))


def reference(tokens, gate_weight, routes, combine, cotangent):
    pairs = TOK_DEV * TOPK
    slices = N_REPLICA
    width = D // N_REPLICA
    sources = N_EXPERT
    ids = routes.reshape(sources, pairs).astype(jnp.int32)
    onehot = (ids[:, :, None] == jnp.arange(EXPERTS, dtype=jnp.int32)[None, None, :]).astype(jnp.int32)
    slot = jnp.sum((jnp.cumsum(onehot, axis=1) - onehot) * onehot, axis=2).astype(jnp.int32)
    source = jnp.broadcast_to(jnp.arange(sources, dtype=jnp.int32)[:, None], (sources, pairs))
    order = jnp.broadcast_to(jnp.arange(pairs, dtype=jnp.int32)[None, :], (sources, pairs))
    table = jnp.full((EXPERTS, sources, CAP), pairs, jnp.int32).at[ids, source, slot].set(order)
    flat_cot = cotangent.reshape(TOKENS * TOPK, HW)
    flat_w = combine.reshape(TOKENS * TOPK)
    src_col = jnp.arange(sources, dtype=jnp.int32)[:, None]

    def one_expert(carry, inputs):
        expert_table, weight = inputs
        valid = expert_table < pairs
        token = jnp.minimum(src_col * TOK_DEV + expert_table // TOPK, TOKENS - 1).astype(jnp.int32).reshape(-1)
        pair = jnp.minimum(src_col * pairs + expert_table, TOKENS * TOPK - 1).astype(jnp.int32).reshape(-1)
        mask = valid.reshape(-1)
        rows = jnp.where(mask[:, None], tokens[token], jnp.zeros((), tokens.dtype))
        cot = jnp.where(mask[:, None], flat_cot[pair], jnp.zeros((), cotangent.dtype))
        wts = jnp.where(mask, flat_w[pair], jnp.zeros((), combine.dtype))
        parts = jnp.einsum("srd,rdh->rsh", rows.reshape(-1, slices, width).astype(jnp.float32),
                           weight.reshape(slices, width, HW).astype(jnp.float32))
        rounded = lax.optimization_barrier(parts.astype(jnp.bfloat16))
        gate = jnp.sum(rounded.astype(jnp.float32), axis=0)
        dhid = (cot.astype(jnp.float32) * wts.astype(jnp.float32)[:, None] * silu_slope(gate)).astype(jnp.bfloat16)
        grad_w = jnp.dot(rows.T, dhid, preferred_element_type=jnp.float32).astype(jnp.bfloat16)
        back = jnp.dot(dhid, weight.T, preferred_element_type=jnp.float32).astype(jnp.bfloat16)
        carry = carry.at[token].add(jnp.where(mask[:, None], back.astype(jnp.float32), jnp.zeros((), jnp.float32)))
        return carry, grad_w

    start = jnp.zeros((TOKENS, D), jnp.float32)
    total, grads = lax.scan(one_expert, start, (table, gate_weight))
    return total.astype(jnp.bfloat16), grads
```

```python
import jax
import jax.numpy as jnp
from jax import lax
from jax.experimental import pallas as pl
from jax.experimental.pallas import tpu as pltpu
from jax.sharding import PartitionSpec as P

MESH = pl.DeviceIdType.MESH


def silu_slope(gate):
    sig = jax.nn.sigmoid(gate)
    return sig * (1.0 + gate * (1.0 - sig))


def local_routed(tokens, gate_weight, routes, combine, cotangent):
    n_exp = lax.axis_size("expert")
    tok_rows = tokens.shape[0]
    width = tokens.shape[1]
    topk = routes.shape[1]
    share = cotangent.shape[2]
    pairs = tok_rows * topk
    cap = max(2, pairs * 5 // (4 * n_exp))
    ids = routes.reshape(pairs)
    onehot = (ids[:, None] == jnp.arange(n_exp, dtype=jnp.int32)[None, :]).astype(jnp.int32)
    slot = jnp.sum((jnp.cumsum(onehot, axis=0) - onehot) * onehot, axis=1)
    target = ids * cap + slot
    slot_pair = (
        jnp.full((n_exp * cap,), pairs, jnp.int32)
        .at[target]
        .set(jnp.arange(pairs, dtype=jnp.int32))
    )
    x_pad = jnp.concatenate([tokens, jnp.zeros((1, width), tokens.dtype)], axis=0)
    cot_pad = jnp.concatenate(
        [cotangent.reshape(pairs, share), jnp.zeros((1, share), cotangent.dtype)], axis=0
    )
    w_pad = jnp.concatenate([combine.reshape(pairs), jnp.zeros((1,), combine.dtype)], axis=0)
    send_x = x_pad[slot_pair // topk].reshape(n_exp, cap, width)
    send_c = cot_pad[slot_pair].reshape(n_exp, cap, share)
    send_w = w_pad[slot_pair].reshape(n_exp, cap)
    recv_x, recv_c, recv_w = (
        lax.all_to_all(send_x, "expert", split_axis=0, concat_axis=0, tiled=True),
        lax.all_to_all(send_c, "expert", split_axis=0, concat_axis=0, tiled=True),
        lax.all_to_all(send_w, "expert", split_axis=0, concat_axis=0, tiled=True),
    )
    rows = n_exp * cap
    recv_x = recv_x.reshape(rows, width)
    recv_c = recv_c.reshape(rows, share)
    recv_w = recv_w.reshape(rows).astype(jnp.float32)
    weight = gate_weight[0]
    gate_part = jnp.dot(recv_x, weight, preferred_element_type=jnp.float32)
    gate_all = lax.psum(gate_part.astype(jnp.bfloat16), "replica").astype(jnp.float32)
    cot_all = lax.all_gather(recv_c, "replica", axis=1, tiled=True)
    dhid = (cot_all.astype(jnp.float32) * recv_w[:, None] * silu_slope(gate_all)).astype(
        jnp.bfloat16
    )
    back_sum = lax.dot_general(
        dhid, weight, (((1,), (1,)), ((), ())), preferred_element_type=jnp.float32
    )
    grad_sum = lax.dot_general(
        recv_x, dhid, (((0,), (0,)), ((), ())), preferred_element_type=jnp.float32
    )
    back_rows = back_sum.astype(jnp.bfloat16).reshape(n_exp, cap, width)
    arrived = lax.all_to_all(back_rows, "expert", split_axis=0, concat_axis=0, tiled=True).reshape(
        rows, width
    )
    pair_rows = arrived[target].reshape(tok_rows, topk, width)
    token_grad = jnp.sum(pair_rows.astype(jnp.float32), axis=1).astype(jnp.bfloat16)
    return (token_grad, grad_sum.astype(jnp.bfloat16)[None])


LINES = (4, 2, 2)
ORDERS = ((0, 2, 1), (0, 1, 2), (0, 2, 1), (1, 2, 0))
PARTS = len(ORDERS)
STEPS = ((0, -1), (0, 1), (1, 1), (2, 1))


def here():
    me = lax.axis_index("expert")
    return (me // 4, (me // 2) % 2, me % 2)


def index_of(at):
    return (at[0] * 2 + at[1]) * 2 + at[2]


def moved(at, axis, by):
    to = list(at)
    to[axis] = at[axis] + by if axis == 0 else (at[axis] + by) % 2
    return tuple(to)


def inside(at):
    return jnp.logical_and(at[0] >= 0, at[0] < LINES[0])


def branches(order, off):
    last = -1
    for j, axis in enumerate(order):
        if off[axis] != 0:
            last = j
    found = []
    for way, (axis, by) in enumerate(STEPS):
        j = order.index(axis)
        if j > last or (j == last and axis == 0 and by * off[0] < 0):
            found.append(way)
    return found, (order[last] if last >= 0 else None)


def offsets(far_first):
    every = [
        (dz, dy, dx)
        for dz in range(-LINES[0] + 1, LINES[0])
        for dy in range(2)
        for dx in range(2)
    ]
    every.sort(key=lambda d: (abs(d[0]) + d[1] + d[2], abs(d[0])), reverse=far_first)
    return every


def greet(at):
    barrier = pltpu.get_barrier_semaphore()
    for axis, by in STEPS:
        to = moved(at, axis, by)

        @pl.when(inside(to))
        def _(to=to):
            pl.semaphore_signal(
                barrier, inc=1, device_id={"expert": index_of(to)}, device_id_type=MESH
            )

    edge = jnp.logical_or(at[0] == 0, at[0] == LINES[0] - 1)

    @pl.when(edge)
    def _():
        pl.semaphore_wait(barrier, 3)

    @pl.when(jnp.logical_not(edge))
    def _():
        pl.semaphore_wait(barrier, 4)


def spread_kernel(x_ref, all_ref, send_sem, recv_sem, own_sem):
    at = here()
    rows, width = x_ref.shape
    cols = width // PARTS
    greet(at)
    own = pltpu.make_async_copy(
        x_ref, all_ref.at[pl.ds(index_of(at) * rows, rows), :], own_sem
    )
    own.start()

    def hop(part, origin, way, mine):
        axis, by = STEPS[way]
        span = pl.ds(part * cols, cols)
        block = all_ref.at[pl.ds(origin * rows, rows), span]
        return pltpu.make_async_remote_copy(
            src_ref=x_ref.at[:, span] if mine else block,
            dst_ref=block,
            send_sem=send_sem.at[part * 64 + origin * 4 + way],
            recv_sem=recv_sem.at[part * 16 + origin],
            device_id={"expert": index_of(moved(at, axis, by))},
            device_id_type=MESH,
        )

    def each(first):
        for off in offsets(False):
            mine = off == (0, 0, 0)
            src = (at[0] + off[0], (at[1] + off[1]) % 2, (at[2] + off[2]) % 2)

            @pl.when(inside(src))
            def _(off=off, mine=mine, src=src):
                origin = index_of(src)
                for part, order in enumerate(ORDERS):
                    ways, _ = branches(order, off)
                    if first and not mine:
                        hop(part, origin, 0, mine).wait_recv()
                    for way in ways:
                        axis, by = STEPS[way]

                        def act(way=way):
                            copy = hop(part, origin, way, mine)
                            copy.start() if first else copy.wait_send()

                        if axis == 0:
                            pl.when(inside(moved(at, axis, by)))(act)
                        else:
                            act()

    each(True)
    each(False)
    own.wait()


def spread_all(tokens):
    rows, width = tokens.shape
    return pl.pallas_call(
        spread_kernel,
        out_shape=jax.ShapeDtypeStruct((16 * rows, width), tokens.dtype),
        in_specs=[pl.BlockSpec(memory_space=pltpu.VMEM)],
        out_specs=pl.BlockSpec(memory_space=pl.ANY),
        scratch_shapes=[
            pltpu.SemaphoreType.DMA((PARTS * 64,)),
            pltpu.SemaphoreType.DMA((PARTS * 16,)),
            pltpu.SemaphoreType.DMA,
        ],
        compiler_params=pltpu.CompilerParams(collective_id=0, has_side_effects=True),
        name="spread_all",
    )(tokens)


def slot_plan():
    bases, total = [], 0
    for order in ORDERS:
        row = []
        for axis, by in STEPS:
            row.append(total)
            count = LINES[0] if axis == 0 else 1
            for other in order[: order.index(axis)]:
                count *= LINES[other]
            total += count
        bases.append(row)
    return bases, total


def collect_kernel(b_ref, out_ref, buf, land, send_sem, recv_sem, own_sem):
    at = here()
    rows, width = out_ref.shape
    cols = width // PARTS
    bases, _ = slot_plan()
    own = pltpu.make_async_copy(b_ref, buf, own_sem)
    own.start()
    greet(at)
    own.wait()

    def slot_of(part, dest, way):
        order = ORDERS[part]
        axis = STEPS[way][0]
        place = 0
        for other in order[: order.index(axis)]:
            place = place * LINES[other] + dest[other]
        if axis == 0:
            place = place * LINES[0] + dest[0]
        return bases[part][way] + place

    def pieces(act):
        for off in offsets(True):
            dest = (at[0] + off[0], (at[1] + off[1]) % 2, (at[2] + off[2]) % 2)

            @pl.when(inside(dest))
            def _(off=off, dest=dest):
                for part in range(PARTS):
                    act(part, off, dest)

    def parent_copy(part, off, dest):
        _, axis = branches(ORDERS[part], off)
        by = 1 if axis != 0 or off[0] > 0 else -1
        back_way = {(0, 1): 0, (0, -1): 1, (1, 1): 2, (2, 1): 3}[(axis, by)]
        slot = slot_of(part, dest, back_way)
        home = index_of(dest)
        return pltpu.make_async_remote_copy(
            src_ref=buf.at[pl.ds(home * rows, rows), pl.ds(part * cols, cols)],
            dst_ref=land.at[slot],
            send_sem=send_sem.at[part * 16 + home],
            recv_sem=recv_sem.at[slot],
            device_id={"expert": index_of(moved(at, axis, by))},
            device_id_type=MESH,
        )

    def gather_in(part, off, dest):
        ways, _ = branches(ORDERS[part], off)
        home = index_of(dest)
        span = pl.ds(part * cols, cols)
        for way in ways:
            axis, by = STEPS[way]

            def take(way=way, axis=axis, by=by):
                slot = slot_of(part, dest, way)
                pltpu.make_async_remote_copy(
                    src_ref=land.at[slot],
                    dst_ref=land.at[slot],
                    send_sem=recv_sem.at[slot],
                    recv_sem=recv_sem.at[slot],
                    device_id={"expert": index_of(moved(at, axis, by))},
                    device_id_type=MESH,
                ).wait_recv()

                def add(i, carry):
                    r = pl.multiple_of(i * 32, 32)
                    line = pl.ds(pl.multiple_of(home * rows + r, 32), 32)
                    buf[line, span] = (
                        buf[line, span].astype(jnp.float32)
                        + land[slot, pl.ds(r, 32), :].astype(jnp.float32)
                    ).astype(jnp.bfloat16)
                    return carry

                lax.fori_loop(0, rows // 32, add, 0)

            if axis == 0:
                pl.when(inside(moved(at, axis, by)))(take)
            else:
                take()

    def work(part, off, dest):
        gather_in(part, off, dest)
        if off != (0, 0, 0):
            parent_copy(part, off, dest).start()

    pieces(work)
    mine = pl.ds(pl.multiple_of(index_of(at) * rows, rows), rows)
    out_ref[...] = buf[mine, :]

    def finish(part, off, dest):
        if off != (0, 0, 0):
            parent_copy(part, off, dest).wait_send()

    pieces(finish)


def collect(back):
    total, width = back.shape
    rows = total // 16
    slots = slot_plan()[1]
    return pl.pallas_call(
        collect_kernel,
        out_shape=jax.ShapeDtypeStruct((rows, width), back.dtype),
        in_specs=[pl.BlockSpec(memory_space=pl.ANY)],
        out_specs=pl.BlockSpec(memory_space=pltpu.VMEM),
        scratch_shapes=[
            pltpu.VMEM((total, width), jnp.bfloat16),
            pltpu.VMEM((slots, rows, width // PARTS), jnp.bfloat16),
            pltpu.SemaphoreType.DMA((PARTS * 16,)),
            pltpu.SemaphoreType.DMA((slots,)),
            pltpu.SemaphoreType.DMA,
        ],
        compiler_params=pltpu.CompilerParams(
            collective_id=1, has_side_effects=True, vmem_limit_bytes=56 * 2**20
        ),
        name="collect",
    )(back)


def local_dense(tokens, gate_weight, routes, combine, cotangent):
    n_exp = lax.axis_size("expert")
    me = lax.axis_index("expert")
    tok_rows, width = tokens.shape
    topk = routes.shape[1]
    hidden = gate_weight.shape[2]
    share = cotangent.shape[2]
    pairs = tok_rows * topk
    cap = max(2, pairs * 5 // (4 * n_exp))
    weight = gate_weight[0]
    routes_all = lax.all_gather(routes, "expert", axis=0, tiled=True)

    earlier = jnp.tril(jnp.ones((tok_rows, tok_rows), jnp.bfloat16), -1)
    onehot = routes[:, :, None] == jnp.arange(n_exp, dtype=jnp.int32)[None, None, :]
    named = jnp.any(onehot, axis=1).astype(jnp.bfloat16)
    rank = jnp.dot(earlier, named, preferred_element_type=jnp.float32)
    slot = jnp.sum(jnp.where(onehot, rank[:, None, :], 0.0), axis=2).astype(jnp.int32)
    target = (routes * cap + slot).reshape(pairs)
    pick = jnp.where(
        jnp.arange(n_exp * cap, dtype=jnp.int32)[:, None] == target[None, :],
        combine.reshape(pairs)[None, :],
        jnp.zeros((), combine.dtype),
    )
    send_c = jnp.dot(
        pick, cotangent.reshape(pairs, share), preferred_element_type=jnp.float32
    ).astype(jnp.bfloat16)
    recv_c = lax.all_to_all(
        send_c.reshape(n_exp, cap, share), "expert", split_axis=0, concat_axis=0, tiled=True
    )
    recv_c = lax.all_gather(recv_c, "replica", axis=2, tiled=True)

    mine = jnp.any(routes_all == me, axis=1).reshape(n_exp, tok_rows)
    place = lax.dot_general(
        mine.astype(jnp.bfloat16), earlier, (((1,), (1,)), ((), ())),
        preferred_element_type=jnp.float32,
    )
    place = jnp.where(mine, place, -1.0).astype(jnp.int32)
    spread = (
        place[:, :, None] == jnp.arange(cap, dtype=jnp.int32)[None, None, :]
    ).astype(jnp.bfloat16)
    cot = lax.dot_general(
        spread, recv_c, (((2,), (1,)), ((0,), (0,))), preferred_element_type=jnp.float32
    ).astype(jnp.bfloat16).reshape(n_exp * tok_rows, hidden)

    x_all = spread_all(tokens)
    gate_part = jnp.dot(x_all, weight, preferred_element_type=jnp.float32)
    gate_all = lax.psum(gate_part.astype(jnp.bfloat16), "replica").astype(jnp.float32)
    dhid = (cot.astype(jnp.float32) * silu_slope(gate_all)).astype(jnp.bfloat16)
    back = lax.dot_general(
        dhid, weight, (((1,), (1,)), ((), ())), preferred_element_type=jnp.float32
    ).astype(jnp.bfloat16)
    token_grad = collect(back)
    grad = lax.dot_general(
        x_all, dhid, (((0,), (0,)), ((), ())), preferred_element_type=jnp.float32
    ).astype(jnp.bfloat16)
    return (token_grad, grad[None])


def local(tokens, gate_weight, routes, combine, cotangent):
    dense = lax.axis_size("expert") == 16 and tokens.shape[1] % 512 == 0
    body = local_dense if dense else local_routed
    return body(tokens, gate_weight, routes, combine, cotangent)


def solution(mesh):
    return jax.shard_map(
        local,
        mesh=mesh,
        in_specs=(
            P("expert", "replica"),
            P("expert", "replica", None),
            P("expert", None),
            P("expert", None),
            P("expert", None, "replica"),
        ),
        out_specs=(P("expert", "replica"), P("expert", "replica", None)),
        check_vma=False,
    )
```

```python
import jax
import jax.numpy as jnp
from jax import lax
from jax.experimental import pallas as pl
from jax.experimental.pallas import tpu as pltpu
from jax.sharding import PartitionSpec as P

MESH = pl.DeviceIdType.MESH


def silu_slope(gate):
    sig = jax.nn.sigmoid(gate)
    return sig * (1.0 + gate * (1.0 - sig))


def local_routed(tokens, gate_weight, routes, combine, cotangent):
    n_exp = lax.axis_size("expert")
    tok_rows = tokens.shape[0]
    width = tokens.shape[1]
    topk = routes.shape[1]
    share = cotangent.shape[2]
    pairs = tok_rows * topk
    cap = max(2, pairs * 5 // (4 * n_exp))
    ids = routes.reshape(pairs)
    onehot = (ids[:, None] == jnp.arange(n_exp, dtype=jnp.int32)[None, :]).astype(jnp.int32)
    slot = jnp.sum((jnp.cumsum(onehot, axis=0) - onehot) * onehot, axis=1)
    target = ids * cap + slot
    slot_pair = (
        jnp.full((n_exp * cap,), pairs, jnp.int32)
        .at[target]
        .set(jnp.arange(pairs, dtype=jnp.int32))
    )
    x_pad = jnp.concatenate([tokens, jnp.zeros((1, width), tokens.dtype)], axis=0)
    cot_pad = jnp.concatenate(
        [cotangent.reshape(pairs, share), jnp.zeros((1, share), cotangent.dtype)], axis=0
    )
    w_pad = jnp.concatenate([combine.reshape(pairs), jnp.zeros((1,), combine.dtype)], axis=0)
    send_x = x_pad[slot_pair // topk].reshape(n_exp, cap, width)
    send_c = cot_pad[slot_pair].reshape(n_exp, cap, share)
    send_w = w_pad[slot_pair].reshape(n_exp, cap)
    recv_x, recv_c, recv_w = (
        lax.all_to_all(send_x, "expert", split_axis=0, concat_axis=0, tiled=True),
        lax.all_to_all(send_c, "expert", split_axis=0, concat_axis=0, tiled=True),
        lax.all_to_all(send_w, "expert", split_axis=0, concat_axis=0, tiled=True),
    )
    rows = n_exp * cap
    recv_x = recv_x.reshape(rows, width)
    recv_c = recv_c.reshape(rows, share)
    recv_w = recv_w.reshape(rows).astype(jnp.float32)
    weight = gate_weight[0]
    gate_part = jnp.dot(recv_x, weight, preferred_element_type=jnp.float32)
    gate_all = lax.psum(gate_part.astype(jnp.bfloat16), "replica").astype(jnp.float32)
    cot_all = lax.all_gather(recv_c, "replica", axis=1, tiled=True)
    dhid = (cot_all.astype(jnp.float32) * recv_w[:, None] * silu_slope(gate_all)).astype(
        jnp.bfloat16
    )
    back_sum = lax.dot_general(
        dhid, weight, (((1,), (1,)), ((), ())), preferred_element_type=jnp.float32
    )
    grad_sum = lax.dot_general(
        recv_x, dhid, (((0,), (0,)), ((), ())), preferred_element_type=jnp.float32
    )
    back_rows = back_sum.astype(jnp.bfloat16).reshape(n_exp, cap, width)
    arrived = lax.all_to_all(back_rows, "expert", split_axis=0, concat_axis=0, tiled=True).reshape(
        rows, width
    )
    pair_rows = arrived[target].reshape(tok_rows, topk, width)
    token_grad = jnp.sum(pair_rows.astype(jnp.float32), axis=1).astype(jnp.bfloat16)
    return (token_grad, grad_sum.astype(jnp.bfloat16)[None])


LINES = (4, 2, 2)
ORDERS = ((0, 2, 1), (0, 1, 2), (0, 2, 1), (1, 2, 0))
PARTS = len(ORDERS)
SWAPS = 4
STEPS = ((0, -1), (0, 1), (1, 1), (2, 1))


def here():
    me = lax.axis_index("expert")
    return (me // 4, (me // 2) % 2, me % 2)


def index_of(at):
    return (at[0] * 2 + at[1]) * 2 + at[2]


def moved(at, axis, by):
    to = list(at)
    to[axis] = at[axis] + by if axis == 0 else (at[axis] + by) % 2
    return tuple(to)


def inside(at):
    return jnp.logical_and(at[0] >= 0, at[0] < LINES[0])


def branches(order, off):
    last = -1
    for j, axis in enumerate(order):
        if off[axis] != 0:
            last = j
    found = []
    for way, (axis, by) in enumerate(STEPS):
        j = order.index(axis)
        if j > last or (j == last and axis == 0 and by * off[0] < 0):
            found.append(way)
    return found, (order[last] if last >= 0 else None)


def offsets(far_first):
    every = [
        (dz, dy, dx)
        for dz in range(-LINES[0] + 1, LINES[0])
        for dy in range(2)
        for dx in range(2)
    ]
    every.sort(key=lambda d: (abs(d[0]) + d[1] + d[2], abs(d[0])), reverse=far_first)
    return every


def greet(at):
    barrier = pltpu.get_barrier_semaphore()
    for axis, by in STEPS:
        to = moved(at, axis, by)

        @pl.when(inside(to))
        def _(to=to):
            pl.semaphore_signal(
                barrier, inc=1, device_id={"expert": index_of(to)}, device_id_type=MESH
            )

    edge = jnp.logical_or(at[0] == 0, at[0] == LINES[0] - 1)

    @pl.when(edge)
    def _():
        pl.semaphore_wait(barrier, 3)

    @pl.when(jnp.logical_not(edge))
    def _():
        pl.semaphore_wait(barrier, 4)


def spread_kernel(x_ref, all_ref, send_sem, recv_sem, own_sem):
    at = here()
    rows, width = x_ref.shape
    cols = width // PARTS
    greet(at)
    own = pltpu.make_async_copy(
        x_ref, all_ref.at[pl.ds(index_of(at) * rows, rows), :], own_sem
    )
    own.start()

    def hop(part, origin, way, mine):
        axis, by = STEPS[way]
        span = pl.ds(part * cols, cols)
        block = all_ref.at[pl.ds(origin * rows, rows), span]
        return pltpu.make_async_remote_copy(
            src_ref=x_ref.at[:, span] if mine else block,
            dst_ref=block,
            send_sem=send_sem.at[part * 64 + origin * 4 + way],
            recv_sem=recv_sem.at[part * 16 + origin],
            device_id={"expert": index_of(moved(at, axis, by))},
            device_id_type=MESH,
        )

    def each(first):
        for off in offsets(False):
            mine = off == (0, 0, 0)
            src = (at[0] + off[0], (at[1] + off[1]) % 2, (at[2] + off[2]) % 2)

            @pl.when(inside(src))
            def _(off=off, mine=mine, src=src):
                origin = index_of(src)
                for part, order in enumerate(ORDERS):
                    ways, _ = branches(order, off)
                    if first and not mine:
                        hop(part, origin, 0, mine).wait_recv()
                    for way in ways:
                        axis, by = STEPS[way]

                        def act(way=way):
                            copy = hop(part, origin, way, mine)
                            copy.start() if first else copy.wait_send()

                        if axis == 0:
                            pl.when(inside(moved(at, axis, by)))(act)
                        else:
                            act()

    each(True)
    each(False)
    own.wait()


def spread_all(tokens):
    rows, width = tokens.shape
    return pl.pallas_call(
        spread_kernel,
        out_shape=jax.ShapeDtypeStruct((16 * rows, width), tokens.dtype),
        in_specs=[pl.BlockSpec(memory_space=pltpu.VMEM)],
        out_specs=pl.BlockSpec(memory_space=pl.ANY),
        scratch_shapes=[
            pltpu.SemaphoreType.DMA((PARTS * 64,)),
            pltpu.SemaphoreType.DMA((PARTS * 16,)),
            pltpu.SemaphoreType.DMA,
        ],
        compiler_params=pltpu.CompilerParams(collective_id=0, has_side_effects=True),
        name="spread_all",
    )(tokens)


def slot_plan():
    bases, total = [], 0
    for order in ORDERS:
        row = []
        for axis, by in STEPS:
            row.append(total)
            count = LINES[0] if axis == 0 else 1
            for other in order[: order.index(axis)]:
                count *= LINES[other]
            total += count
        bases.append(row)
    return bases, total


def collect_kernel(b_ref, out_ref, buf, land, send_sem, recv_sem, own_sem):
    at = here()
    rows, width = out_ref.shape
    cols = width // PARTS
    bases, _ = slot_plan()
    own = pltpu.make_async_copy(b_ref, buf, own_sem)
    own.start()
    greet(at)
    own.wait()

    def slot_of(part, dest, way):
        order = ORDERS[part]
        axis = STEPS[way][0]
        place = 0
        for other in order[: order.index(axis)]:
            place = place * LINES[other] + dest[other]
        if axis == 0:
            place = place * LINES[0] + dest[0]
        return bases[part][way] + place

    def pieces(act):
        for off in offsets(True):
            dest = (at[0] + off[0], (at[1] + off[1]) % 2, (at[2] + off[2]) % 2)

            @pl.when(inside(dest))
            def _(off=off, dest=dest):
                for part in range(PARTS):
                    act(part, off, dest)

    def parent_copy(part, off, dest):
        _, axis = branches(ORDERS[part], off)
        by = 1 if axis != 0 or off[0] > 0 else -1
        back_way = {(0, 1): 0, (0, -1): 1, (1, 1): 2, (2, 1): 3}[(axis, by)]
        slot = slot_of(part, dest, back_way)
        home = index_of(dest)
        return pltpu.make_async_remote_copy(
            src_ref=buf.at[pl.ds(home * rows, rows), pl.ds(part * cols, cols)],
            dst_ref=land.at[slot],
            send_sem=send_sem.at[part * 16 + home],
            recv_sem=recv_sem.at[slot],
            device_id={"expert": index_of(moved(at, axis, by))},
            device_id_type=MESH,
        )

    def gather_in(part, off, dest):
        ways, _ = branches(ORDERS[part], off)
        home = index_of(dest)
        span = pl.ds(part * cols, cols)
        for way in ways:
            axis, by = STEPS[way]

            def take(way=way, axis=axis, by=by):
                slot = slot_of(part, dest, way)
                pltpu.make_async_remote_copy(
                    src_ref=land.at[slot],
                    dst_ref=land.at[slot],
                    send_sem=recv_sem.at[slot],
                    recv_sem=recv_sem.at[slot],
                    device_id={"expert": index_of(moved(at, axis, by))},
                    device_id_type=MESH,
                ).wait_recv()

                def add(i, carry):
                    r = pl.multiple_of(i * 32, 32)
                    line = pl.ds(pl.multiple_of(home * rows + r, 32), 32)
                    buf[line, span] = (
                        buf[line, span].astype(jnp.float32)
                        + land[slot, pl.ds(r, 32), :].astype(jnp.float32)
                    ).astype(jnp.bfloat16)
                    return carry

                lax.fori_loop(0, rows // 32, add, 0)

            if axis == 0:
                pl.when(inside(moved(at, axis, by)))(take)
            else:
                take()

    def work(part, off, dest):
        gather_in(part, off, dest)
        if off != (0, 0, 0):
            parent_copy(part, off, dest).start()

    pieces(work)
    mine = pl.ds(pl.multiple_of(index_of(at) * rows, rows), rows)
    out_ref[...] = buf[mine, :]

    def finish(part, off, dest):
        if off != (0, 0, 0):
            parent_copy(part, off, dest).wait_send()

    pieces(finish)


def collect(back):
    total, width = back.shape
    rows = total // 16
    slots = slot_plan()[1]
    return pl.pallas_call(
        collect_kernel,
        out_shape=jax.ShapeDtypeStruct((rows, width), back.dtype),
        in_specs=[pl.BlockSpec(memory_space=pl.ANY)],
        out_specs=pl.BlockSpec(memory_space=pltpu.VMEM),
        scratch_shapes=[
            pltpu.VMEM((total, width), jnp.bfloat16),
            pltpu.VMEM((slots, rows, width // PARTS), jnp.bfloat16),
            pltpu.SemaphoreType.DMA((PARTS * 16,)),
            pltpu.SemaphoreType.DMA((slots,)),
            pltpu.SemaphoreType.DMA,
        ],
        compiler_params=pltpu.CompilerParams(
            collective_id=1, has_side_effects=True, vmem_limit_bytes=56 * 2**20
        ),
        name="collect",
    )(back)


def swap_kernel(a_ref, c_ref, oa_ref, oc_ref, send_sem, recv_sem):
    partner = {"replica": 1 - lax.axis_index("replica")}
    barrier = pltpu.get_barrier_semaphore()
    pl.semaphore_signal(barrier, inc=1, device_id=partner, device_id_type=MESH)
    pl.semaphore_wait(barrier, 1)
    copies = []
    for src, dst in ((c_ref, oc_ref), (a_ref, oa_ref)):
        rows = src.shape[0] // SWAPS
        for i in range(SWAPS):
            n = len(copies)
            copies.append(
                pltpu.make_async_remote_copy(
                    src_ref=src.at[pl.ds(i * rows, rows), :],
                    dst_ref=dst.at[pl.ds(i * rows, rows), :],
                    send_sem=send_sem.at[n],
                    recv_sem=recv_sem.at[n],
                    device_id=partner,
                    device_id_type=MESH,
                )
            )
    for copy in copies:
        copy.start()
    for copy in copies:
        copy.wait()


def swap(a, c):
    return pl.pallas_call(
        swap_kernel,
        out_shape=(
            jax.ShapeDtypeStruct(a.shape, a.dtype),
            jax.ShapeDtypeStruct(c.shape, c.dtype),
        ),
        in_specs=[pl.BlockSpec(memory_space=pl.ANY)] * 2,
        out_specs=[pl.BlockSpec(memory_space=pl.ANY)] * 2,
        scratch_shapes=[
            pltpu.SemaphoreType.DMA((2 * SWAPS,)),
            pltpu.SemaphoreType.DMA((2 * SWAPS,)),
        ],
        compiler_params=pltpu.CompilerParams(collective_id=2, has_side_effects=True),
        name="swap",
    )(a, c)


def weight_sum_kernel(x_ref, d_ref, o_ref):
    o_ref[...] = lax.dot_general(
        x_ref[...], d_ref[...], (((0,), (0,)), ((), ())), preferred_element_type=jnp.float32
    ).astype(o_ref.dtype)


def weight_sum(x_all, dhid):
    total, width = x_all.shape
    hidden = dhid.shape[1]
    return pl.pallas_call(
        weight_sum_kernel,
        out_shape=jax.ShapeDtypeStruct((width, hidden), jnp.bfloat16),
        grid=(width // 512,),
        in_specs=[
            pl.BlockSpec((total, 512), lambda i: (0, i)),
            pl.BlockSpec((total, hidden), lambda i: (0, 0)),
        ],
        out_specs=pl.BlockSpec((512, hidden), lambda i: (i, 0)),
        compiler_params=pltpu.CompilerParams(vmem_limit_bytes=48 * 2**20),
        name="weight_sum",
    )(x_all, dhid)


def local_dense(tokens, gate_weight, routes, combine, cotangent):
    n_exp = lax.axis_size("expert")
    tok_rows, width = tokens.shape
    topk = routes.shape[1]
    share = cotangent.shape[2]
    pairs = tok_rows * topk
    cap = max(2, pairs * 5 // (4 * n_exp))
    weight = gate_weight[0]
    earlier = jnp.tril(jnp.ones((tok_rows, tok_rows), jnp.bfloat16), -1)
    onehot = routes[:, :, None] == jnp.arange(n_exp, dtype=jnp.int32)[None, None, :]
    named = jnp.any(onehot, axis=1).astype(jnp.bfloat16)
    rank = jnp.dot(earlier, named, preferred_element_type=jnp.float32)
    slot = jnp.sum(jnp.where(onehot, rank[:, None, :], 0.0), axis=2).astype(jnp.int32)
    target = (routes * cap + slot).reshape(pairs)
    taken = jnp.arange(n_exp * cap, dtype=jnp.int32)[:, None] == target[None, :]
    pick = jnp.where(taken, combine.reshape(pairs)[None, :], jnp.zeros((), combine.dtype))
    send_c = jnp.dot(
        pick, cotangent.reshape(pairs, share), preferred_element_type=jnp.float32
    ).astype(jnp.bfloat16)
    token_of = jnp.broadcast_to(
        (jnp.arange(pairs, dtype=jnp.int32) // topk)[:, None], (pairs, 128)
    ).astype(jnp.bfloat16)
    send_t = jnp.dot(
        taken.astype(jnp.bfloat16), token_of, preferred_element_type=jnp.float32
    ).astype(jnp.bfloat16)
    recv = lax.all_to_all(
        jnp.concatenate([send_c, send_t], axis=1).reshape(n_exp, cap, share + 128),
        "expert", split_axis=0, concat_axis=0, tiled=True,
    )

    x_all = spread_all(tokens)
    gate_part = jnp.dot(x_all, weight, preferred_element_type=jnp.float32)
    gate_part = gate_part.astype(jnp.bfloat16)
    spread = (
        recv[:, :, share].astype(jnp.int32)[:, None, :]
        == jnp.arange(tok_rows, dtype=jnp.int32)[None, :, None]
    ).astype(jnp.bfloat16)
    cot = lax.dot_general(
        spread, recv[:, :, :share], (((2,), (1,)), ((0,), (0,))),
        preferred_element_type=jnp.float32,
    ).astype(jnp.bfloat16).reshape(n_exp * tok_rows, share)
    gate_other, cot_other = swap(gate_part, cot)
    gate_all = gate_part.astype(jnp.float32) + gate_other.astype(jnp.float32)
    cot = jnp.where(
        lax.axis_index("replica") == 0,
        jnp.concatenate([cot, cot_other], axis=1),
        jnp.concatenate([cot_other, cot], axis=1),
    )
    dhid = (cot.astype(jnp.float32) * silu_slope(gate_all)).astype(jnp.bfloat16)
    back = lax.dot_general(
        dhid, weight, (((1,), (1,)), ((), ())), preferred_element_type=jnp.float32
    ).astype(jnp.bfloat16)
    token_grad = collect(back)
    grad = weight_sum(x_all, dhid)
    return (token_grad, grad[None])


def local(tokens, gate_weight, routes, combine, cotangent):
    dense = (
        lax.axis_size("expert") == 16
        and lax.axis_size("replica") == 2
        and tokens.shape[0] == 128
        and tokens.shape[1] % 512 == 0
    )
    body = local_dense if dense else local_routed
    return body(tokens, gate_weight, routes, combine, cotangent)


def solution(mesh):
    return jax.shard_map(
        local,
        mesh=mesh,
        in_specs=(
            P("expert", "replica"),
            P("expert", "replica", None),
            P("expert", None),
            P("expert", None),
            P("expert", None, "replica"),
        ),
        out_specs=(P("expert", "replica"), P("expert", "replica", None)),
        check_vma=False,
    )
```
